32 devices in a mesh: groups: 2 (over y), ctx: 4 (over z), head: 2 (over x), dp: 2 (over core).
Axes of the slice: x: 2, y: 2, z: 4, core: 2. Of those that a mesh axis runs over, the one named last changes fastest.
Arguments:
- queries: bfloat16 [4, 4, 512, 16, 128], P(('groups', 'dp'), 'ctx', None, 'head'), parts along dimension 0, may hold values from -6 to 6
- key_vecs: bfloat16 [4, 4, 512, 16, 128], P(('groups', 'dp'), 'ctx', None, 'head'), parts along dimension 0, may hold values from -6 to 6
- value_vecs: bfloat16 [4, 4, 512, 16, 128], P(('groups', 'dp'), 'ctx', None, 'head'), parts along dimension 0, may hold values from -6 to 6
- grad_out: bfloat16 [4, 4, 512, 16, 128], P(('groups', 'dp'), 'ctx', None, 'head'), parts along dimension 0, may hold values from -6 to 6
Outputs:
- attended: bfloat16 [4, 4, 512, 16, 128], P(('groups', 'dp'), 'ctx', None, 'head'), parts along dimension 0
- grad_queries: bfloat16 [4, 4, 512, 16, 128], P(('groups', 'dp'), 'ctx', None, 'head'), parts along dimension 0
- grad_keys: bfloat16 [4, 4, 512, 16, 128], P(('groups', 'dp'), 'ctx', None, 'head'), parts along dimension 0
- grad_values: bfloat16 [4, 4, 512, 16, 128], P(('groups', 'dp'), 'ctx', None, 'head'), parts along dimension 0
The draws below stay inside these ranges and needn't reach their ends.
There are 2 independent parts, one for each index of `groups`. The reference program is written for one: setup_inputs(seed, part) draws one part's arguments, and reference() takes and returns one part's arrays. A program takes and returns all parts, laid end to end along the dimension named above; each array names one. Nothing has to cross between parts.
All inputs are finite; a program needn't handle non-finite values.
Results may differ from the reference program's by a relative error of at most 0.013.
Values may be sent and summed in bfloat16 or wider, within the bound.
A program may use at most 128 MiB of HBM per device.

```python
import math
import jax
import jax.numpy as jnp
from jax import lax

HEADS = 16
HEAD_DIM = 128
COLS = 512
ROWS = 4
BATCH = 2


def draw_queries(key, part):
    shape = (BATCH, ROWS, COLS, HEADS, HEAD_DIM)
    values = jnp.clip(jax.random.normal(jax.random.fold_in(key, 11), shape, jnp.float32), -6.0, 6.0)
    return values.astype(jnp.bfloat16)


def draw_key_vecs(key, part):
    shape = (BATCH, ROWS, COLS, HEADS, HEAD_DIM)
    values = jnp.clip(jax.random.normal(jax.random.fold_in(key, 21), shape, jnp.float32), -6.0, 6.0)
    return values.astype(jnp.bfloat16)


def shard_levels(stream_key, shape, cuts, least, high):
    factor_of = 1.0
    for axis_at, parts in cuts:
        draws = jax.random.uniform(jax.random.fold_in(jax.random.fold_in(stream_key, 6), axis_at), (parts,), jnp.float32, least / len(cuts), high / len(cuts))
        factor_of = factor_of * jnp.repeat(jnp.exp(draws), shape[axis_at] // parts).reshape((-1,) + (1,) * (len(shape) - 1 - axis_at))
    return factor_of


def centred(rng, shape, width, limit, cuts=(), kind=jnp.bfloat16):
    drawn = width * jax.random.normal(rng, shape, jnp.float32)
    if cuts:
        drawn = drawn * shard_levels(rng, shape, cuts, -0.22, 0.18)
    return jnp.clip(drawn, -limit, limit).astype(kind)


def setup_inputs(seed: int = 0, part: int = 0) -> dict:
    seeds = jax.random.split(jax.random.key(seed), 5)
    part_keys = jax.random.split(jax.random.fold_in(seeds[4], part), 5)
    return {
        "queries": draw_queries(jax.random.fold_in(jax.random.fold_in(seeds[4], part), 71), part),
        "key_vecs": draw_key_vecs(jax.random.fold_in(jax.random.fold_in(seeds[4], part), 71), part),
        "value_vecs": centred(part_keys[2], (BATCH, ROWS, COLS, HEADS, HEAD_DIM), 1.0, 6.0, ((0, 2), (1, 4), (3, 2))),
        "grad_out": centred(part_keys[3], (BATCH, ROWS, COLS, HEADS, HEAD_DIM), 1.0, 6.0, ((0, 2), (1, 4), (3, 2))),
    }


def causal(length):
    positions = jnp.arange(length)
    return positions[None, :] <= positions[:, None]

def attend(query_in, key_in, value_in, grad_in, layout, allowed):
    scaling = 1.0 / math.sqrt(HEAD_DIM)
    key_form = layout.replace('q', 'k')
    query_f = query_in.astype(jnp.float32)
    key_f = key_in.astype(jnp.float32)
    value_f = value_in.astype(jnp.float32)
    grad_f = grad_in.astype(jnp.float32)
    scores = jnp.einsum(layout + ',' + key_form + '->bxhqk', query_f, key_f) * scaling
    scores = jnp.where(allowed, scores, -1e+30)
    highest = lax.optimization_barrier(jnp.max(scores, axis=-1, keepdims=True))
    weight_sum = lax.optimization_barrier(jnp.sum(jnp.exp(scores - highest), axis=-1, keepdims=True))
    log_total = highest + jnp.log(weight_sum)
    weights = jnp.where(allowed, jnp.exp(scores - log_total), 0.0)
    rounded = lax.optimization_barrier(weights.astype(jnp.bfloat16)).astype(jnp.float32)
    output = jnp.einsum('bxhqk,' + key_form + '->' + layout, rounded, value_f).astype(jnp.bfloat16)
    output_f = lax.optimization_barrier(output).astype(jnp.float32)
    row_dots = jnp.einsum(layout + ',' + layout + '->bxhq', grad_f, output_f)
    dprobs = jnp.einsum(layout + ',' + key_form + '->bxhqk', grad_f, value_f)
    dscores = (weights * (dprobs - row_dots[..., None]) * scaling).astype(jnp.bfloat16)
    dscores = lax.optimization_barrier(dscores).astype(jnp.float32)
    grad_query = jnp.einsum('bxhqk,' + key_form + '->' + layout, dscores, key_f).astype(jnp.bfloat16)
    grad_key = jnp.einsum('bxhqk,' + layout + '->' + key_form, dscores, query_f).astype(jnp.bfloat16)
    grad_value = jnp.einsum('bxhqk,' + layout + '->' + key_form, rounded, grad_f).astype(jnp.bfloat16)
    return (output, grad_query, grad_key, grad_value)

def merge_heads(first_part, second_part):
    stacked = jnp.stack((first_part, second_part), axis=4)
    shape = first_part.shape
    return stacked.reshape(shape[:3] + (2 * shape[3], shape[4]))

def row_block(pieces):
    widened = tuple((piece[:, None] for piece in pieces))
    results = attend(widened[0], widened[1], widened[2], widened[3], 'bxqhd', causal(COLS))
    return tuple((result[:, 0] for result in results))

def reference(queries, key_vecs, value_vecs, grad_out):
    arrays = (queries, key_vecs, value_vecs, grad_out)
    row_parts = tuple((jnp.moveaxis(array[:, :, :, 0::2], 1, 0) for array in arrays))
    col_parts = tuple((array[:, :, :, 1::2] for array in arrays))
    row_results = lax.map(row_block, row_parts)
    row_results = tuple((jnp.moveaxis(result, 0, 1) for result in row_results))
    col_results = attend(col_parts[0], col_parts[1], col_parts[2], col_parts[3], 'bqxhd', causal(ROWS))
    return (merge_heads(row_results[0], col_results[0]), merge_heads(row_results[1], col_results[1]), merge_heads(row_results[2], col_results[2]), merge_heads(row_results[3], col_results[3]))
```

```python
import functools
import math

import jax
import jax.numpy as jnp
from jax import lax
from jax.experimental import pallas as pl
from jax.experimental.pallas import tpu as pltpu
from jax.sharding import PartitionSpec as P

MESH = pl.DeviceIdType.MESH
F32 = jnp.float32
BF16 = jnp.bfloat16
NT = (((1,), (1,)), ((), ()))
NN = (((1,), (0,)), ((), ()))
TN = (((0,), (0,)), ((), ()))


def mm(a, b, dims):
    return lax.dot_general(a, b, dims, preferred_element_type=F32)


def row_head(buf, stage, i, tokens, depth):
    scaling = 1.0 / math.sqrt(depth)
    block = tokens // 2
    keys = buf[i, 1]
    values = buf[i, 2]
    parts = []
    for b in (1, 0):
        rows = pl.ds(b * block, block)
        span = (b + 1) * block
        q = buf[i, 0, rows]
        g = buf[i, 3, rows]
        k = keys[:span]
        v = values[:span]
        s = mm(q, k, NT) * scaling
        qpos = lax.broadcasted_iota(jnp.int32, (block, span), 0) + b * block
        kpos = lax.broadcasted_iota(jnp.int32, (block, span), 1)
        s = jnp.where(kpos <= qpos, s, -1e30)
        top = jnp.max(s, axis=-1, keepdims=True)
        e = jnp.exp(s - top)
        p = e * (1.0 / jnp.sum(e, axis=-1, keepdims=True))
        pb = p.astype(BF16)
        o = mm(pb, v, NN).astype(BF16).astype(F32)
        dots = jnp.sum(g.astype(F32) * o, axis=-1, keepdims=True)
        dp = mm(g, v, NT)
        ds = (p * (dp - dots) * scaling).astype(BF16)
        stage[0, 2 * i, rows] = o
        stage[1, 2 * i, rows] = mm(ds, k, NN)
        dk = mm(ds, q, TN)
        dv = mm(pb, g, TN)
        if b == 1:
            stage[2, 2 * i] = dk
            stage[3, 2 * i] = dv
        else:
            stage[2, 2 * i, pl.ds(0, span)] += dk
            stage[3, 2 * i, pl.ds(0, span)] += dv


def column_block(queries, keys, scaling):
    outs = []
    grads = [None] * len(keys)
    for q, g, seen in queries:
        s = [jnp.sum(q * k, axis=-1, keepdims=True) * scaling for k, _ in keys[:seen]]
        dp = [jnp.sum(g * v, axis=-1, keepdims=True) for _, v in keys[:seen]]
        top = functools.reduce(jnp.maximum, s)
        e = [jnp.exp(x - top) for x in s]
        inverse = 1.0 / functools.reduce(jnp.add, e)
        p = [x * inverse for x in e]
        dots = functools.reduce(jnp.add, [x * y for x, y in zip(p, dp)])
        ds = [x * (y - dots) * scaling for x, y in zip(p, dp)]
        o = functools.reduce(jnp.add, [x * kv[1] for x, kv in zip(p, keys)])
        dq = functools.reduce(jnp.add, [x * kv[0] for x, kv in zip(ds, keys)])
        outs.append((o, dq))
        for j in range(seen):
            dk, dv = ds[j] * q, p[j] * g
            grads[j] = (dk, dv) if grads[j] is None else (grads[j][0] + dk, grads[j][1] + dv)
    return outs, grads


def kernel(
    q_ref, k_ref, v_ref, g_ref, o_out, dq_out, dk_out, dv_out,
    wide, rows_in, cols_in, stage, in_a, in_b, in_c, ret_a, ret_b, ret_c,
    sent1, got_a, got_b, got_c, sent2, back_a, back_b, back_c,
):
    tokens, local_heads, depth = q_ref.shape
    heads = local_heads // 2
    scaling = 1.0 / math.sqrt(depth)
    me = lax.axis_index("ctx")
    barrier = pltpu.get_barrier_semaphore()
    for step in range(1, 4):
        pl.semaphore_signal(
            barrier, inc=1, device_id={"ctx": lax.rem(me + step, 4)}, device_id_type=MESH
        )

    def remote(src, dst, send, recv, target):
        return pltpu.make_async_remote_copy(
            src_ref=src, dst_ref=dst, send_sem=send, recv_sem=recv,
            device_id={"ctx": target}, device_id_type=MESH,
        )

    def kv_to(i, target, buf, got, slot):
        return remote(cols_in.at[i, pl.ds(1, 2)], buf.at[i], sent1.at[slot, i], got.at[i], target)

    def all_to(i):
        return remote(cols_in.at[i], in_c.at[i], sent1.at[0, i], got_c.at[i], 2)

    CH = 64
    chunks = tokens // CH

    def split(ref, at):
        def widen(c, _):
            x = ref[pl.ds(c * CH, CH)].astype(F32)
            wide[pl.ds(c * CH * local_heads, CH * local_heads)] = x.reshape(CH * local_heads, depth)
            return 0

        lax.fori_loop(0, chunks, widen, 0)

        def pick(c, _):
            for h in range(local_heads):
                x = wide[pl.ds(c * CH * local_heads + h, CH, stride=local_heads)].astype(BF16)
                buf = rows_in if h % 2 == 0 else cols_in
                buf[h // 2, at, pl.ds(c * CH, CH)] = x
            return 0

        lax.fori_loop(0, chunks, pick, 0)

    split(k_ref, 1)
    split(v_ref, 2)
    pl.semaphore_wait(barrier, 3)

    def each(count, body):
        def step(i, _):
            body(i)
            return 0

        lax.fori_loop(0, count, step, 0)

    @pl.when(me == 0)
    def _():
        def go(i):
            kv_to(i, 2, in_a, got_a, 0).start()
            kv_to(i, 1, in_a, got_a, 1).start()

        each(heads, go)

    @pl.when(me == 1)
    def _():
        each(heads, lambda i: kv_to(i, 2, in_b, got_b, 0).start())

    split(q_ref, 0)
    split(g_ref, 3)

    @pl.when(me == 3)
    def _():
        each(heads, lambda i: all_to(i).start())

    def ret_a_copy(i, src, target, slot):
        return remote(src.at[i], ret_a.at[i], sent2.at[slot, i], back_a.at[i], target)

    def ret_b_copy(i):
        return remote(in_a.at[i], ret_b.at[i], sent2.at[0, i], back_b.at[i], 0)

    def ret_c_copy(i):
        return remote(in_c.at[i], ret_c.at[i], sent2.at[2, i], back_c.at[i], 3)

    CB = 128

    def own(i, rows):
        return [cols_in[i, a, rows].astype(F32) for a in range(4)]

    def put_own(i, rows, out, grad):
        stage[0, 2 * i + 1, rows] = out[0]
        stage[1, 2 * i + 1, rows] = out[1]
        stage[2, 2 * i + 1, rows] = grad[0]
        stage[3, 2 * i + 1, rows] = grad[1]

    def pair(buf, i, rows):
        return (buf[i, 0, rows].astype(F32), buf[i, 1, rows].astype(F32))

    def put_pair(buf, i, rows, grad):
        buf[i, 0, rows] = grad[0].astype(BF16)
        buf[i, 1, rows] = grad[1].astype(BF16)

    def body(i):
        row_head(rows_in, stage, i, tokens, depth)

        @pl.when(me == 0)
        def _():
            def block(c):
                rows = pl.ds(c * CB, CB)
                q, k, v, g = own(i, rows)
                outs, grads = column_block([(q, g, 1)], [(k, v)], scaling)
                put_own(i, rows, outs[0], grads[0])

            each(tokens // CB, block)

        @pl.when(me == 1)
        def _():
            kv_to(i, 1, in_a, got_a, 1).wait_recv()

            def block(c):
                rows = pl.ds(c * CB, CB)
                q, k, v, g = own(i, rows)
                outs, grads = column_block([(q, g, 2)], [pair(in_a, i, rows), (k, v)], scaling)
                put_own(i, rows, outs[0], grads[1])
                put_pair(in_a, i, rows, grads[0])

            each(tokens // CB, block)
            ret_a_copy(i, in_a, 0, 0).start()

        @pl.when(me == 2)
        def _():
            kv_to(i, 2, in_a, got_a, 0).wait_recv()
            kv_to(i, 2, in_b, got_b, 0).wait_recv()
            all_to(i).wait_recv()

            def block(c):
                rows = pl.ds(c * CB, CB)
                q, k, v, g = own(i, rows)
                q3, k3, v3, g3 = [in_c[i, a, rows].astype(F32) for a in range(4)]
                outs, grads = column_block(
                    [(q, g, 3), (q3, g3, 4)],
                    [pair(in_a, i, rows), pair(in_b, i, rows), (k, v), (k3, v3)],
                    scaling,
                )
                put_own(i, rows, outs[0], grads[2])
                put_pair(in_a, i, rows, grads[0])
                put_pair(in_b, i, rows, grads[1])
                for a, x in enumerate(outs[1] + grads[3]):
                    in_c[i, a, rows] = x.astype(BF16)

            each(tokens // CB, block)
            ret_b_copy(i).start()
            ret_a_copy(i, in_b, 1, 1).start()
            ret_c_copy(i).start()

    each(heads, body)

    def join(at, ref):
        def spread(c):
            for h in range(local_heads):
                wide[pl.ds(c * CH * local_heads + h, CH, stride=local_heads)] = stage[
                    at, h, pl.ds(c * CH, CH)
                ]

        each(chunks, spread)

        def narrow(c):
            x = wide[pl.ds(c * CH * local_heads, CH * local_heads)]
            ref[pl.ds(c * CH, CH)] = x.reshape(CH, local_heads, depth).astype(BF16)

        each(chunks, narrow)

    def add(i, at, x):
        stage[at, 2 * i + 1] += x.astype(F32)

    @pl.when(me == 3)
    def _():
        def take(i):
            ret_c_copy(i).wait_recv()
            for a in range(4):
                stage[a, 2 * i + 1] = ret_c[i, a].astype(F32)

        each(heads, take)

    join(0, o_out)
    join(1, dq_out)

    @pl.when(me == 0)
    def _():
        def take(i):
            ret_a_copy(i, in_a, 0, 0).wait_recv()
            ret_b_copy(i).wait_recv()
            for a in range(2):
                add(i, 2 + a, ret_a[i, a].astype(F32) + ret_b[i, a].astype(F32))

        each(heads, take)

    @pl.when(me == 1)
    def _():
        def take(i):
            ret_a_copy(i, in_b, 1, 1).wait_recv()
            for a in range(2):
                add(i, 2 + a, ret_a[i, a])

        each(heads, take)

    join(2, dk_out)
    join(3, dv_out)

    @pl.when(me == 0)
    def _():
        def done(i):
            kv_to(i, 2, in_a, got_a, 0).wait_send()
            kv_to(i, 1, in_a, got_a, 1).wait_send()

        each(heads, done)

    @pl.when(me == 1)
    def _():
        def done(i):
            kv_to(i, 2, in_b, got_b, 0).wait_send()
            ret_a_copy(i, in_a, 0, 0).wait_send()

        each(heads, done)

    @pl.when(me == 2)
    def _():
        def done(i):
            ret_b_copy(i).wait_send()
            ret_a_copy(i, in_b, 1, 1).wait_send()
            ret_c_copy(i).wait_send()

        each(heads, done)

    @pl.when(me == 3)
    def _():
        each(heads, lambda i: all_to(i).wait_send())


def fused(queries, key_vecs, value_vecs, grad_out):
    shape = queries.shape
    tokens, local_heads, depth = shape[2:]
    heads = local_heads // 2
    flat = [x.reshape(tokens, local_heads, depth) for x in (queries, key_vecs, value_vecs, grad_out)]
    vmem = pl.BlockSpec(memory_space=pltpu.VMEM)
    two = pltpu.VMEM((heads, 2, tokens, depth), BF16)
    four = pltpu.VMEM((heads, 4, tokens, depth), BF16)
    dma = pltpu.SemaphoreType.DMA
    results = pl.pallas_call(
        kernel,
        out_shape=[jax.ShapeDtypeStruct((tokens, local_heads, depth), BF16)] * 4,
        in_specs=[vmem] * 4,
        out_specs=[vmem] * 4,
        scratch_shapes=[
            pltpu.VMEM((tokens * local_heads, depth), F32),
            four, four,
            pltpu.VMEM((4, local_heads, tokens, depth), F32),
            two, two, four, two, two, four,
            dma((2, heads)), dma((heads,)), dma((heads,)), dma((heads,)),
            dma((3, heads)), dma((heads,)), dma((heads,)), dma((heads,)),
        ],
        compiler_params=pltpu.CompilerParams(
            collective_id=0, has_side_effects=True, vmem_limit_bytes=56 * 1024 * 1024
        ),
    )(*flat)
    return tuple(x.reshape(shape) for x in results)


def causal(length):
    positions = jnp.arange(length)
    return positions[None, :] <= positions[:, None]


def attend(query_in, key_in, value_in, grad_in, layout, allowed):
    scaling = 1.0 / math.sqrt(query_in.shape[-1])
    key_form = layout.replace("q", "k")
    scores = (
        jnp.einsum(
            layout + "," + key_form + "->bxhqk",
            query_in,
            key_in,
            preferred_element_type=jnp.float32,
        )
        * scaling
    )
    scores = jnp.where(allowed, scores, -1e30)
    highest = jnp.max(scores, axis=-1, keepdims=True)
    weight_sum = jnp.sum(jnp.exp(scores - highest), axis=-1, keepdims=True)
    log_total = highest + jnp.log(weight_sum)
    weights = jnp.where(allowed, jnp.exp(scores - log_total), 0.0)
    rounded = weights.astype(jnp.bfloat16)
    output = jnp.einsum(
        "bxhqk," + key_form + "->" + layout, rounded, value_in, preferred_element_type=jnp.float32
    ).astype(jnp.bfloat16)
    row_dots = jnp.einsum(
        layout + "," + layout + "->bxhq", grad_in, output, preferred_element_type=jnp.float32
    )
    dprobs = jnp.einsum(
        layout + "," + key_form + "->bxhqk", grad_in, value_in, preferred_element_type=jnp.float32
    )
    dscores = (weights * (dprobs - row_dots[..., None]) * scaling).astype(jnp.bfloat16)
    grad_query = jnp.einsum(
        "bxhqk," + key_form + "->" + layout, dscores, key_in, preferred_element_type=jnp.float32
    ).astype(jnp.bfloat16)
    grad_key = jnp.einsum(
        "bxhqk," + layout + "->" + key_form, dscores, query_in, preferred_element_type=jnp.float32
    )
    grad_value = jnp.einsum(
        "bxhqk," + layout + "->" + key_form, rounded, grad_in, preferred_element_type=jnp.float32
    )
    return (output, grad_query, grad_key, grad_value)


def merge_heads(first_part, second_part):
    stacked = jnp.stack((first_part, second_part), axis=4)
    shape = first_part.shape
    return stacked.reshape(shape[:3] + (2 * shape[3], shape[4]))


def per_device(queries, key_vecs, value_vecs, grad_out):
    arrays = (queries, key_vecs, value_vecs, grad_out)
    row_parts = tuple((array[:, :, :, 0::2] for array in arrays))
    col_parts = tuple((array[:, :, :, 1::2] for array in arrays))
    row_local = attend(
        row_parts[0], row_parts[1], row_parts[2], row_parts[3], "bxqhd", causal(queries.shape[2])
    )
    row_results = (
        row_local[0],
        row_local[1],
        row_local[2].astype(jnp.bfloat16),
        row_local[3].astype(jnp.bfloat16),
    )
    local_rows = col_parts[0].shape[1]
    gathered = (
        lax.all_gather(col_parts[1], "ctx", axis=1, tiled=True),
        lax.all_gather(col_parts[2], "ctx", axis=1, tiled=True),
    )
    query_rows = lax.axis_index("ctx") * local_rows + jnp.arange(local_rows)
    key_rows = jnp.arange(gathered[0].shape[1])
    allowed = key_rows[None, :] <= query_rows[:, None]
    col_local = attend(col_parts[0], gathered[0], gathered[1], col_parts[3], "bqxhd", allowed)
    summed = (
        lax.psum_scatter(col_local[2], "ctx", scatter_dimension=1, tiled=True),
        lax.psum_scatter(col_local[3], "ctx", scatter_dimension=1, tiled=True),
    )
    col_results = (
        col_local[0],
        col_local[1],
        summed[0].astype(jnp.bfloat16),
        summed[1].astype(jnp.bfloat16),
    )
    return (
        merge_heads(row_results[0], col_results[0]),
        merge_heads(row_results[1], col_results[1]),
        merge_heads(row_results[2], col_results[2]),
        merge_heads(row_results[3], col_results[3]),
    )


def solution(mesh):
    body = fused if mesh.shape["ctx"] == 4 else per_device
    placed = (
        P(("groups", "dp"), "ctx", None, "head", None),
        P(("groups", "dp"), "ctx", None, "head", None),
        P(("groups", "dp"), "ctx", None, "head", None),
        P(("groups", "dp"), "ctx", None, "head", None),
    )
    return jax.shard_map(
        body,
        mesh=mesh,
        in_specs=placed,
        out_specs=(
            P(("groups", "dp"), "ctx", None, "head", None),
            P(("groups", "dp"), "ctx", None, "head", None),
            P(("groups", "dp"), "ctx", None, "head", None),
            P(("groups", "dp"), "ctx", None, "head", None),
        ),
        check_vma=False,
    )
```

```python
import functools
import math

import jax
import jax.numpy as jnp
from jax import lax
from jax.experimental import pallas as pl
from jax.experimental.pallas import tpu as pltpu
from jax.sharding import PartitionSpec as P

MESH = pl.DeviceIdType.MESH
F32 = jnp.float32
BF16 = jnp.bfloat16
NT = (((1,), (1,)), ((), ()))
NN = (((1,), (0,)), ((), ()))
TN = (((0,), (0,)), ((), ()))


def mm(a, b, dims):
    return lax.dot_general(a, b, dims, preferred_element_type=F32)


def row_piece(buf, acc, stage, i, b, tokens, depth):
    scaling = 1.0 / math.sqrt(depth)
    block = tokens // 2
    rows = pl.ds(b * block, block)
    span = (b + 1) * block
    q = buf[i, 0, rows]
    g = buf[i, 3, rows]
    k = buf[i, 1, pl.ds(0, span)]
    v = buf[i, 2, pl.ds(0, span)]
    s = mm(q, k, NT) * scaling
    qpos = lax.broadcasted_iota(jnp.int32, (block, span), 0) + b * block
    kpos = lax.broadcasted_iota(jnp.int32, (block, span), 1)
    s = jnp.where(kpos <= qpos, s, -1e30)
    top = jnp.max(s, axis=-1, keepdims=True)
    e = jnp.exp(s - top)
    p = e * (1.0 / jnp.sum(e, axis=-1, keepdims=True))
    pb = p.astype(BF16)
    o = mm(pb, v, NN).astype(BF16)
    dots = jnp.sum(g.astype(F32) * o.astype(F32), axis=-1, keepdims=True)
    dp = mm(g, v, NT)
    ds = (p * (dp - dots) * scaling).astype(BF16)
    stage[i, 0, rows] = o
    stage[i, 1, rows] = mm(ds, k, NN).astype(BF16)
    dk = mm(ds, q, TN)
    dv = mm(pb, g, TN)
    if b == 1:
        acc[0] = dk[:block]
        acc[1] = dv[:block]
        stage[i, 2, rows] = dk[block:].astype(BF16)
        stage[i, 3, rows] = dv[block:].astype(BF16)
    else:
        stage[i, 2, rows] = (acc[0] + dk).astype(BF16)
        stage[i, 3, rows] = (acc[1] + dv).astype(BF16)


def column_block(queries, keys, scaling):
    outs = []
    grads = [None] * len(keys)
    for q, g, seen in queries:
        s = [jnp.sum(q * k, axis=-1, keepdims=True) * scaling for k, _ in keys[:seen]]
        dp = [jnp.sum(g * v, axis=-1, keepdims=True) for _, v in keys[:seen]]
        top = functools.reduce(jnp.maximum, s)
        e = [jnp.exp(x - top) for x in s]
        inverse = 1.0 / functools.reduce(jnp.add, e)
        p = [x * inverse for x in e]
        dots = functools.reduce(jnp.add, [x * y for x, y in zip(p, dp)])
        ds = [x * (y - dots) * scaling for x, y in zip(p, dp)]
        o = functools.reduce(jnp.add, [x * kv[1] for x, kv in zip(p, keys)])
        dq = functools.reduce(jnp.add, [x * kv[0] for x, kv in zip(ds, keys)])
        outs.append((o, dq))
        for j in range(seen):
            dk, dv = ds[j] * q, p[j] * g
            grads[j] = (dk, dv) if grads[j] is None else (grads[j][0] + dk, grads[j][1] + dv)
    return outs, grads


QUARTERS = 4


def each(count, body):
    def step(i, _):
        body(i)
        return 0

    lax.fori_loop(0, count, step, 0)


def kernel(
    q_ref, k_ref, v_ref, g_ref, rows_out, cols_out,
    fetched, wide, rows_in, cols_in, rows_stage, cols_stage, acc, own_grads,
    in_a, in_b, in_c, ret_a, ret_b, ret_c,
    load, sent1, got_a, got_b, got_c, sent2, back_a, back_b, back_c, left_rows, left_cols,
):
    tokens, local_heads, depth = q_ref.shape
    heads = local_heads // 2
    columns = tokens // QUARTERS
    chunks = heads * QUARTERS
    scaling = 1.0 / math.sqrt(depth)
    me = lax.axis_index("ctx")
    refs = (q_ref, k_ref, v_ref, g_ref)

    def fetch(at, quarter):
        part = pl.ds(quarter * columns, columns)
        return pltpu.make_async_copy(
            refs[at].at[part], fetched.at[at, part], load.at[at, quarter]
        )

    for quarter in range(QUARTERS):
        for at in (1, 2, 0, 3):
            fetch(at, quarter).start()

    barrier = pltpu.get_barrier_semaphore()
    for step in range(1, 4):
        pl.semaphore_signal(
            barrier, inc=1, device_id={"ctx": lax.rem(me + step, 4)}, device_id_type=MESH
        )

    def remote(src, dst, send, recv, target):
        return pltpu.make_async_remote_copy(
            src_ref=src, dst_ref=dst, send_sem=send, recv_sem=recv,
            device_id={"ctx": target}, device_id_type=MESH,
        )

    def kv_to(c, target, buf, got, slot):
        return remote(cols_in.at[c, pl.ds(1, 2)], buf.at[c], sent1.at[slot, c], got.at[c], target)

    def all_to(c):
        return remote(cols_in.at[c], in_c.at[c], sent1.at[0, c], got_c.at[c], 2)

    def split(at, quarter):
        fetch(at, quarter).wait()
        x = fetched[at, pl.ds(quarter * columns, columns)].astype(F32)
        wide[at] = x.reshape(columns * local_heads, depth)
        for h in range(local_heads):
            x = wide[at, pl.ds(h, columns, stride=local_heads)].astype(BF16)
            if h % 2 == 0:
                rows_in[h // 2, at, pl.ds(quarter * columns, columns)] = x
            else:
                cols_in[quarter * heads + h // 2, at] = x

    pl.semaphore_wait(barrier, 3)

    def prepare(quarter):
        split(1, quarter)
        split(2, quarter)

        @pl.when(me == 0)
        def _():
            def go(i):
                kv_to(quarter * heads + i, 2, in_a, got_a, 0).start()
                kv_to(quarter * heads + i, 1, in_a, got_a, 1).start()

            each(heads, go)

        @pl.when(me == 1)
        def _():
            each(heads, lambda i: kv_to(quarter * heads + i, 2, in_b, got_b, 0).start())

        split(0, quarter)
        split(3, quarter)

        @pl.when(me == 3)
        def _():
            each(heads, lambda i: all_to(quarter * heads + i).start())

    each(QUARTERS, prepare)

    def ret_a_copy(c, src, target, slot):
        return remote(src.at[c], ret_a.at[c], sent2.at[slot, c], back_a.at[c], target)

    def ret_b_copy(c):
        return remote(in_a.at[c], ret_b.at[c], sent2.at[0, c], back_b.at[c], 0)

    def ret_c_copy(c):
        return remote(in_c.at[c], ret_c.at[c], sent2.at[2, c], back_c.at[c], 3)

    def rows_leave(i):
        return pltpu.make_async_copy(rows_stage.at[i], rows_out.at[i], left_rows.at[i])

    def cols_leave(c):
        return pltpu.make_async_copy(cols_stage.at[c], cols_out.at[c], left_cols.at[c])

    def own(c):
        return [cols_in[c, a].astype(F32) for a in range(4)]

    def put(ref, c, first, values):
        for a, x in enumerate(values):
            ref[c, first + a] = x.astype(ref.dtype)

    def pair(buf, c):
        return (buf[c, 0].astype(F32), buf[c, 1].astype(F32))

    def body(c):
        @pl.when(c % QUARTERS == 0)
        def _():
            row_piece(rows_in, acc, rows_stage, c // QUARTERS, 1, tokens, depth)

        @pl.when(c % QUARTERS == 2)
        def _():
            row_piece(rows_in, acc, rows_stage, c // QUARTERS, 0, tokens, depth)
            rows_leave(c // QUARTERS).start()

        @pl.when(me == 0)
        def _():
            q, k, v, g = own(c)
            outs, grads = column_block([(q, g, 1)], [(k, v)], scaling)
            put(cols_stage, c, 0, outs[0])
            put(own_grads, c, 0, grads[0])

        @pl.when(me == 1)
        def _():
            kv_to(c, 1, in_a, got_a, 1).wait_recv()
            q, k, v, g = own(c)
            outs, grads = column_block([(q, g, 2)], [pair(in_a, c), (k, v)], scaling)
            put(in_a, c, 0, grads[0])
            ret_a_copy(c, in_a, 0, 0).start()
            put(cols_stage, c, 0, outs[0])
            put(own_grads, c, 0, grads[1])

        @pl.when(me == 2)
        def _():
            kv_to(c, 2, in_a, got_a, 0).wait_recv()
            kv_to(c, 2, in_b, got_b, 0).wait_recv()
            all_to(c).wait_recv()
            q, k, v, g = own(c)
            q3, k3, v3, g3 = [in_c[c, a].astype(F32) for a in range(4)]
            outs, grads = column_block(
                [(q, g, 3), (q3, g3, 4)],
                [pair(in_a, c), pair(in_b, c), (k, v), (k3, v3)],
                scaling,
            )
            put(in_a, c, 0, grads[0])
            put(in_b, c, 0, grads[1])
            put(in_c, c, 0, outs[1] + grads[3])
            ret_b_copy(c).start()
            ret_a_copy(c, in_b, 1, 1).start()
            ret_c_copy(c).start()
            put(cols_stage, c, 0, outs[0] + grads[2])
            cols_leave(c).start()

    each(chunks, body)

    @pl.when(me == 0)
    def _():
        def take(c):
            ret_a_copy(c, in_a, 0, 0).wait_recv()
            ret_b_copy(c).wait_recv()
            total = [
                own_grads[c, a] + ret_a[c, a].astype(F32) + ret_b[c, a].astype(F32)
                for a in range(2)
            ]
            put(cols_stage, c, 2, total)
            cols_leave(c).start()

        each(chunks, take)

    @pl.when(me == 1)
    def _():
        def take(c):
            ret_a_copy(c, in_b, 1, 1).wait_recv()
            put(cols_stage, c, 2, [own_grads[c, a] + ret_a[c, a].astype(F32) for a in range(2)])
            cols_leave(c).start()

        each(chunks, take)

    @pl.when(me == 3)
    def _():
        def take(c):
            ret_c_copy(c).wait_recv()
            cols_stage[c] = ret_c[c]
            cols_leave(c).start()

        each(chunks, take)

    each(heads, lambda i: rows_leave(i).wait())
    each(chunks, lambda c: cols_leave(c).wait())

    @pl.when(me == 0)
    def _():
        def done(c):
            kv_to(c, 2, in_a, got_a, 0).wait_send()
            kv_to(c, 1, in_a, got_a, 1).wait_send()

        each(chunks, done)

    @pl.when(me == 1)
    def _():
        def done(c):
            kv_to(c, 2, in_b, got_b, 0).wait_send()
            ret_a_copy(c, in_a, 0, 0).wait_send()

        each(chunks, done)

    @pl.when(me == 2)
    def _():
        def done(c):
            ret_b_copy(c).wait_send()
            ret_a_copy(c, in_b, 1, 1).wait_send()
            ret_c_copy(c).wait_send()

        each(chunks, done)

    @pl.when(me == 3)
    def _():
        each(chunks, lambda c: all_to(c).wait_send())


def join_kernel(rows_ref, cols_ref, o_out, dq_out, dk_out, dv_out, wide):
    columns, local_heads, depth = o_out.shape
    for a, out in enumerate((o_out, dq_out, dk_out, dv_out)):
        for h in range(local_heads):
            x = rows_ref[h // 2, a] if h % 2 == 0 else cols_ref[h // 2, a]
            wide[a, pl.ds(h, columns, stride=local_heads)] = x.astype(F32)
        out[...] = wide[a].reshape(columns, local_heads, depth).astype(BF16)


def fused(queries, key_vecs, value_vecs, grad_out):
    shape = queries.shape
    tokens, local_heads, depth = shape[2:]
    heads = local_heads // 2
    columns = tokens // QUARTERS
    chunks = heads * QUARTERS
    flat = [x.reshape(tokens, local_heads, depth) for x in (queries, key_vecs, value_vecs, grad_out)]
    anywhere = pl.BlockSpec(memory_space=pl.ANY)
    two = pltpu.VMEM((chunks, 2, columns, depth), BF16)
    four = pltpu.VMEM((chunks, 4, columns, depth), BF16)
    row_buf = pltpu.VMEM((heads, 4, tokens, depth), BF16)
    dma = pltpu.SemaphoreType.DMA
    rows, cols = pl.pallas_call(
        kernel,
        out_shape=[
            jax.ShapeDtypeStruct((heads, 4, tokens, depth), BF16),
            jax.ShapeDtypeStruct((chunks, 4, columns, depth), BF16),
        ],
        in_specs=[anywhere] * 4,
        out_specs=[anywhere] * 2,
        scratch_shapes=[
            pltpu.VMEM((4, tokens, local_heads, depth), BF16),
            pltpu.VMEM((4, columns * local_heads, depth), F32),
            row_buf, four, row_buf, four,
            pltpu.VMEM((2, tokens // 2, depth), F32),
            pltpu.VMEM((chunks, 2, columns, depth), F32),
            two, two, four, two, two, four,
            dma((4, QUARTERS)),
            dma((2, chunks)), dma((chunks,)), dma((chunks,)), dma((chunks,)),
            dma((3, chunks)), dma((chunks,)), dma((chunks,)), dma((chunks,)),
            dma((heads,)), dma((chunks,)),
        ],
        compiler_params=pltpu.CompilerParams(
            collective_id=0, has_side_effects=True, vmem_limit_bytes=56 * 1024 * 1024
        ),
    )(*flat)
    results = pl.pallas_call(
        join_kernel,
        grid=(QUARTERS,),
        out_shape=[jax.ShapeDtypeStruct((tokens, local_heads, depth), BF16)] * 4,
        in_specs=[
            pl.BlockSpec((heads, 4, columns, depth), lambda c: (0, 0, c, 0)),
            pl.BlockSpec((heads, 4, columns, depth), lambda c: (c, 0, 0, 0)),
        ],
        out_specs=[pl.BlockSpec((columns, local_heads, depth), lambda c: (c, 0, 0))] * 4,
        scratch_shapes=[pltpu.VMEM((4, columns * local_heads, depth), F32)],
    )(rows, cols)
    return tuple(x.reshape(shape) for x in results)


def causal(length):
    positions = jnp.arange(length)
    return positions[None, :] <= positions[:, None]


def attend(query_in, key_in, value_in, grad_in, layout, allowed):
    scaling = 1.0 / math.sqrt(query_in.shape[-1])
    key_form = layout.replace("q", "k")
    scores = (
        jnp.einsum(
            layout + "," + key_form + "->bxhqk",
            query_in,
            key_in,
            preferred_element_type=jnp.float32,
        )
        * scaling
    )
    scores = jnp.where(allowed, scores, -1e30)
    highest = jnp.max(scores, axis=-1, keepdims=True)
    weight_sum = jnp.sum(jnp.exp(scores - highest), axis=-1, keepdims=True)
    log_total = highest + jnp.log(weight_sum)
    weights = jnp.where(allowed, jnp.exp(scores - log_total), 0.0)
    rounded = weights.astype(jnp.bfloat16)
    output = jnp.einsum(
        "bxhqk," + key_form + "->" + layout, rounded, value_in, preferred_element_type=jnp.float32
    ).astype(jnp.bfloat16)
    row_dots = jnp.einsum(
        layout + "," + layout + "->bxhq", grad_in, output, preferred_element_type=jnp.float32
    )
    dprobs = jnp.einsum(
        layout + "," + key_form + "->bxhqk", grad_in, value_in, preferred_element_type=jnp.float32
    )
    dscores = (weights * (dprobs - row_dots[..., None]) * scaling).astype(jnp.bfloat16)
    grad_query = jnp.einsum(
        "bxhqk," + key_form + "->" + layout, dscores, key_in, preferred_element_type=jnp.float32
    ).astype(jnp.bfloat16)
    grad_key = jnp.einsum(
        "bxhqk," + layout + "->" + key_form, dscores, query_in, preferred_element_type=jnp.float32
    )
    grad_value = jnp.einsum(
        "bxhqk," + layout + "->" + key_form, rounded, grad_in, preferred_element_type=jnp.float32
    )
    return (output, grad_query, grad_key, grad_value)


def merge_heads(first_part, second_part):
    stacked = jnp.stack((first_part, second_part), axis=4)
    shape = first_part.shape
    return stacked.reshape(shape[:3] + (2 * shape[3], shape[4]))


def per_device(queries, key_vecs, value_vecs, grad_out):
    arrays = (queries, key_vecs, value_vecs, grad_out)
    row_parts = tuple((array[:, :, :, 0::2] for array in arrays))
    col_parts = tuple((array[:, :, :, 1::2] for array in arrays))
    row_local = attend(
        row_parts[0], row_parts[1], row_parts[2], row_parts[3], "bxqhd", causal(queries.shape[2])
    )
    row_results = (
        row_local[0],
        row_local[1],
        row_local[2].astype(jnp.bfloat16),
        row_local[3].astype(jnp.bfloat16),
    )
    local_rows = col_parts[0].shape[1]
    gathered = (
        lax.all_gather(col_parts[1], "ctx", axis=1, tiled=True),
        lax.all_gather(col_parts[2], "ctx", axis=1, tiled=True),
    )
    query_rows = lax.axis_index("ctx") * local_rows + jnp.arange(local_rows)
    key_rows = jnp.arange(gathered[0].shape[1])
    allowed = key_rows[None, :] <= query_rows[:, None]
    col_local = attend(col_parts[0], gathered[0], gathered[1], col_parts[3], "bqxhd", allowed)
    summed = (
        lax.psum_scatter(col_local[2], "ctx", scatter_dimension=1, tiled=True),
        lax.psum_scatter(col_local[3], "ctx", scatter_dimension=1, tiled=True),
    )
    col_results = (
        col_local[0],
        col_local[1],
        summed[0].astype(jnp.bfloat16),
        summed[1].astype(jnp.bfloat16),
    )
    return (
        merge_heads(row_results[0], col_results[0]),
        merge_heads(row_results[1], col_results[1]),
        merge_heads(row_results[2], col_results[2]),
        merge_heads(row_results[3], col_results[3]),
    )


def solution(mesh):
    body = fused if mesh.shape["ctx"] == 4 else per_device
    placed = (
        P(("groups", "dp"), "ctx", None, "head", None),
        P(("groups", "dp"), "ctx", None, "head", None),
        P(("groups", "dp"), "ctx", None, "head", None),
        P(("groups", "dp"), "ctx", None, "head", None),
    )
    return jax.shard_map(
        body,
        mesh=mesh,
        in_specs=placed,
        out_specs=(
            P(("groups", "dp"), "ctx", None, "head", None),
            P(("groups", "dp"), "ctx", None, "head", None),
            P(("groups", "dp"), "ctx", None, "head", None),
            P(("groups", "dp"), "ctx", None, "head", None),
        ),
        check_vma=False,
    )
```

```python
import functools
import math

import jax
import jax.numpy as jnp
from jax import lax
from jax.experimental import pallas as pl
from jax.experimental.pallas import tpu as pltpu
from jax.sharding import PartitionSpec as P

MESH = pl.DeviceIdType.MESH
F32 = jnp.float32
BF16 = jnp.bfloat16
NT = (((1,), (1,)), ((), ()))
NN = (((1,), (0,)), ((), ()))
TN = (((0,), (0,)), ((), ()))


def mm(a, b, dims):
    return lax.dot_general(a, b, dims, preferred_element_type=F32)


def row_piece(buf, acc, stage, i, b, tokens, depth):
    scaling = 1.0 / math.sqrt(depth)
    block = tokens // 2
    rows = pl.ds(b * block, block)
    span = (b + 1) * block
    q = buf[i, 0, rows]
    g = buf[i, 3, rows]
    k = buf[i, 1, pl.ds(0, span)]
    v = buf[i, 2, pl.ds(0, span)]
    s = mm(q, k, NT) * scaling
    qpos = lax.broadcasted_iota(jnp.int32, (block, span), 0) + b * block
    kpos = lax.broadcasted_iota(jnp.int32, (block, span), 1)
    s = jnp.where(kpos <= qpos, s, -1e30)
    top = jnp.max(s, axis=-1, keepdims=True)
    e = jnp.exp(s - top)
    p = e * (1.0 / jnp.sum(e, axis=-1, keepdims=True))
    pb = p.astype(BF16)
    o = mm(pb, v, NN).astype(BF16)
    dots = jnp.sum(g.astype(F32) * o.astype(F32), axis=-1, keepdims=True)
    dp = mm(g, v, NT)
    ds = (p * (dp - dots) * scaling).astype(BF16)
    stage[i, 0, rows] = o
    stage[i, 1, rows] = mm(ds, k, NN).astype(BF16)
    dk = mm(ds, q, TN)
    dv = mm(pb, g, TN)
    if b == 1:
        acc[0] = dk[:block]
        acc[1] = dv[:block]
        stage[i, 2, rows] = dk[block:].astype(BF16)
        stage[i, 3, rows] = dv[block:].astype(BF16)
    else:
        stage[i, 2, rows] = (acc[0] + dk).astype(BF16)
        stage[i, 3, rows] = (acc[1] + dv).astype(BF16)


def column_block(queries, keys, scaling):
    outs = []
    grads = [None] * len(keys)
    for q, g, seen in queries:
        s = [jnp.sum(q * k, axis=-1, keepdims=True) * scaling for k, _ in keys[:seen]]
        dp = [jnp.sum(g * v, axis=-1, keepdims=True) for _, v in keys[:seen]]
        top = functools.reduce(jnp.maximum, s)
        e = [jnp.exp(x - top) for x in s]
        inverse = 1.0 / functools.reduce(jnp.add, e)
        p = [x * inverse for x in e]
        dots = functools.reduce(jnp.add, [x * y for x, y in zip(p, dp)])
        ds = [x * (y - dots) * scaling for x, y in zip(p, dp)]
        o = functools.reduce(jnp.add, [x * kv[1] for x, kv in zip(p, keys)])
        dq = functools.reduce(jnp.add, [x * kv[0] for x, kv in zip(ds, keys)])
        outs.append((o, dq))
        for j in range(seen):
            dk, dv = ds[j] * q, p[j] * g
            grads[j] = (dk, dv) if grads[j] is None else (grads[j][0] + dk, grads[j][1] + dv)
    return outs, grads


QUARTERS = 4
PARTS = 1


def each(count, body):
    def step(i, _):
        body(i)
        return 0

    lax.fori_loop(0, count, step, 0)


def kernel(
    q_ref, k_ref, v_ref, g_ref, rows_out, cols_out,
    fetched, wide, rows_in, cols_in, rows_stage, cols_stage, acc, own_grads,
    in_a, in_b, in_c, ret_a, ret_b, ret_c,
    load, sent1, got_a, got_b, got_c, sent2, back_a, back_b, back_c, left_rows, left_cols,
):
    tokens, local_heads, depth = q_ref.shape
    heads = local_heads // 2
    columns = tokens // QUARTERS
    chunks = heads * QUARTERS
    scaling = 1.0 / math.sqrt(depth)
    me = lax.axis_index("ctx")
    refs = (q_ref, k_ref, v_ref, g_ref)

    def fetch(at, quarter):
        part = pl.ds(quarter * columns, columns)
        return pltpu.make_async_copy(
            refs[at].at[part], fetched.at[at, part], load.at[at, quarter]
        )

    for quarter in range(QUARTERS):
        for at in (1, 2, 0, 3):
            fetch(at, quarter).start()

    barrier = pltpu.get_barrier_semaphore()

    def greet(target):
        pl.semaphore_signal(barrier, inc=1, device_id={"ctx": target}, device_id_type=MESH)

    @pl.when(me < 2)
    def _():
        greet(1 - me)
        greet(2)

    @pl.when(me == 2)
    def _():
        greet(0)
        greet(1)
        greet(3)

    @pl.when(me == 3)
    def _():
        greet(2)

    def remote(src, dst, send, recv, target):
        return pltpu.make_async_remote_copy(
            src_ref=src, dst_ref=dst, send_sem=send, recv_sem=recv,
            device_id={"ctx": target}, device_id_type=MESH,
        )

    def kv_to(c, target, buf, got, slot):
        return remote(cols_in.at[c, pl.ds(1, 2)], buf.at[c], sent1.at[slot, c], got.at[c], target)

    def all_to(c):
        return remote(cols_in.at[c], in_c.at[c], sent1.at[0, c], got_c.at[c], 2)

    def split(at, quarter):
        fetch(at, quarter).wait()
        x = fetched[at, pl.ds(quarter * columns, columns)].astype(F32)
        wide[at] = x.reshape(columns * local_heads, depth)
        for h in range(local_heads):
            x = wide[at, pl.ds(h, columns, stride=local_heads)].astype(BF16)
            if h % 2 == 0:
                rows_in[h // 2, at, pl.ds(quarter * columns, columns)] = x
            else:
                cols_in[quarter * heads + h // 2, at] = x

    for at in (1, 2, 0, 3):
        split(at, 0)
    pl.semaphore_wait(barrier, jnp.where(me < 2, 2, jnp.where(me == 2, 3, 1)))

    def prepare(quarter):
        @pl.when(quarter > 0)
        def _():
            split(1, quarter)
            split(2, quarter)

        @pl.when(me == 0)
        def _():
            def go(i):
                kv_to(quarter * heads + i, 2, in_a, got_a, 0).start()
                kv_to(quarter * heads + i, 1, in_a, got_a, 1).start()

            each(heads, go)

        @pl.when(me == 1)
        def _():
            each(heads, lambda i: kv_to(quarter * heads + i, 2, in_b, got_b, 0).start())

        @pl.when(quarter > 0)
        def _():
            split(0, quarter)
            split(3, quarter)

        @pl.when(me == 3)
        def _():
            each(heads, lambda i: all_to(quarter * heads + i).start())

    each(QUARTERS, prepare)

    def ret_a_copy(c, src, target, slot):
        return remote(src.at[c], ret_a.at[c], sent2.at[slot, c], back_a.at[c], target)

    def ret_b_copy(c):
        return remote(in_a.at[c], ret_b.at[c], sent2.at[0, c], back_b.at[c], 0)

    def ret_c_copy(c):
        return remote(in_c.at[c], ret_c.at[c], sent2.at[2, c], back_c.at[c], 3)

    def rows_leave(i):
        return pltpu.make_async_copy(rows_stage.at[i], rows_out.at[i], left_rows.at[i])

    def cols_leave(c):
        return pltpu.make_async_copy(cols_stage.at[c], cols_out.at[c], left_cols.at[c])

    def own(c):
        return [cols_in[c, a].astype(F32) for a in range(4)]

    def put(ref, c, first, values):
        for a, x in enumerate(values):
            ref[c, first + a] = x.astype(ref.dtype)

    def pair(buf, c):
        return (buf[c, 0].astype(F32), buf[c, 1].astype(F32))

    def body(c):
        @pl.when(c % QUARTERS == 0)
        def _():
            row_piece(rows_in, acc, rows_stage, c // QUARTERS, 1, tokens, depth)

        @pl.when(c % QUARTERS == 2)
        def _():
            row_piece(rows_in, acc, rows_stage, c // QUARTERS, 0, tokens, depth)
            rows_leave(c // QUARTERS).start()

        @pl.when(me == 0)
        def _():
            q, k, v, g = own(c)
            outs, grads = column_block([(q, g, 1)], [(k, v)], scaling)
            put(cols_stage, c, 0, outs[0])
            put(own_grads, c, 0, grads[0])

        @pl.when(me == 1)
        def _():
            kv_to(c, 1, in_a, got_a, 1).wait_recv()
            q, k, v, g = own(c)
            outs, grads = column_block([(q, g, 2)], [pair(in_a, c), (k, v)], scaling)
            put(in_a, c, 0, grads[0])
            ret_a_copy(c, in_a, 0, 0).start()
            put(cols_stage, c, 0, outs[0])
            put(own_grads, c, 0, grads[1])

        @pl.when(me == 2)
        def _():
            kv_to(c, 2, in_a, got_a, 0).wait_recv()
            kv_to(c, 2, in_b, got_b, 0).wait_recv()
            all_to(c).wait_recv()
            q, k, v, g = own(c)
            q3, k3, v3, g3 = [in_c[c, a].astype(F32) for a in range(4)]
            outs, grads = column_block(
                [(q, g, 3), (q3, g3, 4)],
                [pair(in_a, c), pair(in_b, c), (k, v), (k3, v3)],
                scaling,
            )
            put(in_a, c, 0, grads[0])
            put(in_b, c, 0, grads[1])
            put(in_c, c, 0, outs[1] + grads[3])
            ret_b_copy(c).start()
            ret_a_copy(c, in_b, 1, 1).start()
            ret_c_copy(c).start()
            put(cols_stage, c, 0, outs[0] + grads[2])
            cols_leave(c).start()

    each(chunks, body)

    @pl.when(me == 0)
    def _():
        def take(c):
            ret_a_copy(c, in_a, 0, 0).wait_recv()
            ret_b_copy(c).wait_recv()
            total = [
                own_grads[c, a] + ret_a[c, a].astype(F32) + ret_b[c, a].astype(F32)
                for a in range(2)
            ]
            put(cols_stage, c, 2, total)
            cols_leave(c).start()

        each(chunks, take)

    @pl.when(me == 1)
    def _():
        def take(c):
            ret_a_copy(c, in_b, 1, 1).wait_recv()
            put(cols_stage, c, 2, [own_grads[c, a] + ret_a[c, a].astype(F32) for a in range(2)])
            cols_leave(c).start()

        each(chunks, take)

    @pl.when(me == 3)
    def _():
        def take(c):
            ret_c_copy(c).wait_recv()
            cols_stage[c] = ret_c[c]
            cols_leave(c).start()

        each(chunks, take)

    each(heads, lambda i: rows_leave(i).wait())
    each(chunks, lambda c: cols_leave(c).wait())

    @pl.when(me == 0)
    def _():
        def done(c):
            kv_to(c, 2, in_a, got_a, 0).wait_send()
            kv_to(c, 1, in_a, got_a, 1).wait_send()

        each(chunks, done)

    @pl.when(me == 1)
    def _():
        def done(c):
            kv_to(c, 2, in_b, got_b, 0).wait_send()
            ret_a_copy(c, in_a, 0, 0).wait_send()

        each(chunks, done)

    @pl.when(me == 2)
    def _():
        def done(c):
            ret_b_copy(c).wait_send()
            ret_a_copy(c, in_b, 1, 1).wait_send()
            ret_c_copy(c).wait_send()

        each(chunks, done)

    @pl.when(me == 3)
    def _():
        each(chunks, lambda c: all_to(c).wait_send())


def join_kernel(rows_ref, cols_ref, o_out, dq_out, dk_out, dv_out, wide):
    columns, local_heads, depth = o_out.shape
    for a, out in enumerate((o_out, dq_out, dk_out, dv_out)):
        for h in range(local_heads):
            x = rows_ref[h // 2, a] if h % 2 == 0 else cols_ref[h // 2, a]
            wide[a, pl.ds(h, columns, stride=local_heads)] = x.astype(F32)
        out[...] = wide[a].reshape(columns, local_heads, depth).astype(BF16)


def fused(queries, key_vecs, value_vecs, grad_out):
    shape = queries.shape
    tokens, local_heads, depth = shape[2:]
    heads = local_heads // 2
    columns = tokens // QUARTERS
    chunks = heads * QUARTERS
    part = columns // PARTS
    flat = [x.reshape(tokens, local_heads, depth) for x in (queries, key_vecs, value_vecs, grad_out)]
    anywhere = pl.BlockSpec(memory_space=pl.ANY)
    two = pltpu.VMEM((chunks, 2, columns, depth), BF16)
    four = pltpu.VMEM((chunks, 4, columns, depth), BF16)
    row_buf = pltpu.VMEM((heads, 4, tokens, depth), BF16)
    dma = pltpu.SemaphoreType.DMA
    rows, cols = pl.pallas_call(
        kernel,
        out_shape=[
            jax.ShapeDtypeStruct((heads, 4, tokens, depth), BF16),
            jax.ShapeDtypeStruct((chunks, 4, columns, depth), BF16),
        ],
        in_specs=[anywhere] * 4,
        out_specs=[anywhere] * 2,
        scratch_shapes=[
            pltpu.VMEM((4, tokens, local_heads, depth), BF16),
            pltpu.VMEM((4, columns * local_heads, depth), F32),
            row_buf, four, row_buf, four,
            pltpu.VMEM((2, tokens // 2, depth), F32),
            pltpu.VMEM((chunks, 2, columns, depth), F32),
            two, two, four, two, two, four,
            dma((4, QUARTERS)),
            dma((2, chunks)), dma((chunks,)), dma((chunks,)), dma((chunks,)),
            dma((3, chunks)), dma((chunks,)), dma((chunks,)), dma((chunks,)),
            dma((heads,)), dma((chunks,)),
        ],
        compiler_params=pltpu.CompilerParams(
            collective_id=0, has_side_effects=True, vmem_limit_bytes=56 * 1024 * 1024
        ),
    )(*flat)
    results = pl.pallas_call(
        join_kernel,
        grid=(QUARTERS * PARTS,),
        out_shape=[jax.ShapeDtypeStruct((tokens, local_heads, depth), BF16)] * 4,
        in_specs=[
            pl.BlockSpec((heads, 4, part, depth), lambda c: (0, 0, c, 0)),
            pl.BlockSpec((heads, 4, part, depth), lambda c: (c // PARTS, 0, c % PARTS, 0)),
        ],
        out_specs=[pl.BlockSpec((part, local_heads, depth), lambda c: (c, 0, 0))] * 4,
        scratch_shapes=[pltpu.VMEM((4, part * local_heads, depth), F32)],
    )(rows, cols)
    return tuple(x.reshape(shape) for x in results)


def causal(length):
    positions = jnp.arange(length)
    return positions[None, :] <= positions[:, None]


def attend(query_in, key_in, value_in, grad_in, layout, allowed):
    scaling = 1.0 / math.sqrt(query_in.shape[-1])
    key_form = layout.replace("q", "k")
    scores = (
        jnp.einsum(
            layout + "," + key_form + "->bxhqk",
            query_in,
            key_in,
            preferred_element_type=jnp.float32,
        )
        * scaling
    )
    scores = jnp.where(allowed, scores, -1e30)
    highest = jnp.max(scores, axis=-1, keepdims=True)
    weight_sum = jnp.sum(jnp.exp(scores - highest), axis=-1, keepdims=True)
    log_total = highest + jnp.log(weight_sum)
    weights = jnp.where(allowed, jnp.exp(scores - log_total), 0.0)
    rounded = weights.astype(jnp.bfloat16)
    output = jnp.einsum(
        "bxhqk," + key_form + "->" + layout, rounded, value_in, preferred_element_type=jnp.float32
    ).astype(jnp.bfloat16)
    row_dots = jnp.einsum(
        layout + "," + layout + "->bxhq", grad_in, output, preferred_element_type=jnp.float32
    )
    dprobs = jnp.einsum(
        layout + "," + key_form + "->bxhqk", grad_in, value_in, preferred_element_type=jnp.float32
    )
    dscores = (weights * (dprobs - row_dots[..., None]) * scaling).astype(jnp.bfloat16)
    grad_query = jnp.einsum(
        "bxhqk," + key_form + "->" + layout, dscores, key_in, preferred_element_type=jnp.float32
    ).astype(jnp.bfloat16)
    grad_key = jnp.einsum(
        "bxhqk," + layout + "->" + key_form, dscores, query_in, preferred_element_type=jnp.float32
    )
    grad_value = jnp.einsum(
        "bxhqk," + layout + "->" + key_form, rounded, grad_in, preferred_element_type=jnp.float32
    )
    return (output, grad_query, grad_key, grad_value)


def merge_heads(first_part, second_part):
    stacked = jnp.stack((first_part, second_part), axis=4)
    shape = first_part.shape
    return stacked.reshape(shape[:3] + (2 * shape[3], shape[4]))


def per_device(queries, key_vecs, value_vecs, grad_out):
    arrays = (queries, key_vecs, value_vecs, grad_out)
    row_parts = tuple((array[:, :, :, 0::2] for array in arrays))
    col_parts = tuple((array[:, :, :, 1::2] for array in arrays))
    row_local = attend(
        row_parts[0], row_parts[1], row_parts[2], row_parts[3], "bxqhd", causal(queries.shape[2])
    )
    row_results = (
        row_local[0],
        row_local[1],
        row_local[2].astype(jnp.bfloat16),
        row_local[3].astype(jnp.bfloat16),
    )
    local_rows = col_parts[0].shape[1]
    gathered = (
        lax.all_gather(col_parts[1], "ctx", axis=1, tiled=True),
        lax.all_gather(col_parts[2], "ctx", axis=1, tiled=True),
    )
    query_rows = lax.axis_index("ctx") * local_rows + jnp.arange(local_rows)
    key_rows = jnp.arange(gathered[0].shape[1])
    allowed = key_rows[None, :] <= query_rows[:, None]
    col_local = attend(col_parts[0], gathered[0], gathered[1], col_parts[3], "bqxhd", allowed)
    summed = (
        lax.psum_scatter(col_local[2], "ctx", scatter_dimension=1, tiled=True),
        lax.psum_scatter(col_local[3], "ctx", scatter_dimension=1, tiled=True),
    )
    col_results = (
        col_local[0],
        col_local[1],
        summed[0].astype(jnp.bfloat16),
        summed[1].astype(jnp.bfloat16),
    )
    return (
        merge_heads(row_results[0], col_results[0]),
        merge_heads(row_results[1], col_results[1]),
        merge_heads(row_results[2], col_results[2]),
        merge_heads(row_results[3], col_results[3]),
    )


def solution(mesh):
    body = fused if mesh.shape["ctx"] == 4 else per_device
    placed = (
        P(("groups", "dp"), "ctx", None, "head", None),
        P(("groups", "dp"), "ctx", None, "head", None),
        P(("groups", "dp"), "ctx", None, "head", None),
        P(("groups", "dp"), "ctx", None, "head", None),
    )
    return jax.shard_map(
        body,
        mesh=mesh,
        in_specs=placed,
        out_specs=(
            P(("groups", "dp"), "ctx", None, "head", None),
            P(("groups", "dp"), "ctx", None, "head", None),
            P(("groups", "dp"), "ctx", None, "head", None),
            P(("groups", "dp"), "ctx", None, "head", None),
        ),
        check_vma=False,
    )
```

```python
import functools
import math

import jax
import jax.numpy as jnp
from jax import lax
from jax.experimental import pallas as pl
from jax.experimental.pallas import tpu as pltpu
from jax.sharding import PartitionSpec as P

MESH = pl.DeviceIdType.MESH
F32 = jnp.float32
BF16 = jnp.bfloat16
NT = (((1,), (1,)), ((), ()))
NN = (((1,), (0,)), ((), ()))
TN = (((0,), (0,)), ((), ()))


def mm(a, b, dims):
    return lax.dot_general(a, b, dims, preferred_element_type=F32)


def row_piece(buf, acc, stage, i, b, tokens, depth):
    scaling = 1.0 / math.sqrt(depth)
    block = tokens // 2
    rows = pl.ds(b * block, block)
    span = (b + 1) * block
    q = buf[i, 0, rows]
    g = buf[i, 3, rows]
    k = buf[i, 1, pl.ds(0, span)]
    v = buf[i, 2, pl.ds(0, span)]
    s = mm(q, k, NT) * scaling
    qpos = lax.broadcasted_iota(jnp.int32, (block, span), 0) + b * block
    kpos = lax.broadcasted_iota(jnp.int32, (block, span), 1)
    s = jnp.where(kpos <= qpos, s, -1e30)
    top = jnp.max(s, axis=-1, keepdims=True)
    e = jnp.exp(s - top)
    p = e * (1.0 / jnp.sum(e, axis=-1, keepdims=True))
    pb = p.astype(BF16)
    o = mm(pb, v, NN).astype(BF16)
    dots = jnp.sum(g.astype(F32) * o.astype(F32), axis=-1, keepdims=True)
    dp = mm(g, v, NT)
    ds = (p * (dp - dots) * scaling).astype(BF16)
    stage[i, 0, rows] = o
    stage[i, 1, rows] = mm(ds, k, NN).astype(BF16)
    dk = mm(ds, q, TN)
    dv = mm(pb, g, TN)
    if b == 1:
        acc[0] = dk[:block]
        acc[1] = dv[:block]
        stage[i, 2, rows] = dk[block:].astype(BF16)
        stage[i, 3, rows] = dv[block:].astype(BF16)
    else:
        stage[i, 2, rows] = (acc[0] + dk).astype(BF16)
        stage[i, 3, rows] = (acc[1] + dv).astype(BF16)


def column_block(queries, keys, scaling):
    outs = []
    grads = [None] * len(keys)
    for q, g, seen in queries:
        s = [jnp.sum(q * k, axis=-1, keepdims=True) * scaling for k, _ in keys[:seen]]
        dp = [jnp.sum(g * v, axis=-1, keepdims=True) for _, v in keys[:seen]]
        top = functools.reduce(jnp.maximum, s)
        e = [jnp.exp(x - top) for x in s]
        inverse = 1.0 / functools.reduce(jnp.add, e)
        p = [x * inverse for x in e]
        dots = functools.reduce(jnp.add, [x * y for x, y in zip(p, dp)])
        ds = [x * (y - dots) * scaling for x, y in zip(p, dp)]
        o = functools.reduce(jnp.add, [x * kv[1] for x, kv in zip(p, keys)])
        dq = functools.reduce(jnp.add, [x * kv[0] for x, kv in zip(ds, keys)])
        outs.append((o, dq))
        for j in range(seen):
            dk, dv = ds[j] * q, p[j] * g
            grads[j] = (dk, dv) if grads[j] is None else (grads[j][0] + dk, grads[j][1] + dv)
    return outs, grads


QUARTERS = 4


def each(count, body):
    def step(i, _):
        body(i)
        return 0

    lax.fori_loop(0, count, step, 0)


def kernel(
    q_ref, k_ref, v_ref, g_ref, rows_out, cols_out,
    fetched, wide, rows_in, cols_in, rows_stage, cols_stage, acc, own_grads,
    in_a, in_b, in_c, ret_a, ret_b, ret_c,
    load, sent1, got_a, got_b, got_c, sent2, back_a, back_b, back_c, left_rows, left_cols,
):
    tokens, local_heads, depth = q_ref.shape
    heads = local_heads // 2
    columns = tokens // QUARTERS
    chunks = heads * QUARTERS
    scaling = 1.0 / math.sqrt(depth)
    me = lax.axis_index("ctx")
    refs = (q_ref, k_ref, v_ref, g_ref)

    def fetch(at, quarter):
        part = pl.ds(quarter * columns, columns)
        return pltpu.make_async_copy(
            refs[at].at[part], fetched.at[at, part], load.at[at, quarter]
        )

    for quarter in range(QUARTERS):
        for at in (1, 2, 0, 3):
            fetch(at, quarter).start()

    barrier = pltpu.get_barrier_semaphore()

    def greet(target):
        pl.semaphore_signal(barrier, inc=1, device_id={"ctx": target}, device_id_type=MESH)

    @pl.when(me < 2)
    def _():
        greet(1 - me)
        greet(2)

    @pl.when(me == 2)
    def _():
        greet(0)
        greet(1)
        greet(3)

    @pl.when(me == 3)
    def _():
        greet(2)

    def remote(src, dst, send, recv, target):
        return pltpu.make_async_remote_copy(
            src_ref=src, dst_ref=dst, send_sem=send, recv_sem=recv,
            device_id={"ctx": target}, device_id_type=MESH,
        )

    def kv_to(c, target, buf, got, slot):
        return remote(cols_in.at[c, pl.ds(1, 2)], buf.at[c], sent1.at[slot, c], got.at[c], target)

    def all_to(c):
        return remote(cols_in.at[c], in_c.at[c], sent1.at[0, c], got_c.at[c], 2)

    def split(at, quarter):
        fetch(at, quarter).wait()
        x = fetched[at, pl.ds(quarter * columns, columns)].astype(F32)
        wide[at] = x.reshape(columns * local_heads, depth)
        for h in range(local_heads):
            x = wide[at, pl.ds(h, columns, stride=local_heads)].astype(BF16)
            if h % 2 == 0:
                rows_in[h // 2, at, pl.ds(quarter * columns, columns)] = x
            else:
                cols_in[quarter * heads + h // 2, at] = x

    for at in (1, 2, 0, 3):
        split(at, 0)
    pl.semaphore_wait(barrier, jnp.where(me < 2, 2, jnp.where(me == 2, 3, 1)))

    def prepare(quarter):
        @pl.when(quarter > 0)
        def _():
            split(1, quarter)
            split(2, quarter)

        @pl.when(me == 0)
        def _():
            def go(i):
                kv_to(quarter * heads + i, 2, in_a, got_a, 0).start()
                kv_to(quarter * heads + i, 1, in_a, got_a, 1).start()

            each(heads, go)

        @pl.when(me == 1)
        def _():
            each(heads, lambda i: kv_to(quarter * heads + i, 2, in_b, got_b, 0).start())

        @pl.when(quarter > 0)
        def _():
            split(0, quarter)
            split(3, quarter)

        @pl.when(me == 3)
        def _():
            each(heads, lambda i: all_to(quarter * heads + i).start())

    each(QUARTERS, prepare)

    def ret_a_copy(c, src, target, slot):
        return remote(src.at[c], ret_a.at[c], sent2.at[slot, c], back_a.at[c], target)

    def ret_b_copy(c):
        return remote(in_a.at[c], ret_b.at[c], sent2.at[0, c], back_b.at[c], 0)

    def ret_c_copy(c):
        return remote(in_c.at[c], ret_c.at[c], sent2.at[2, c], back_c.at[c], 3)

    def rows_leave(i):
        return pltpu.make_async_copy(rows_stage.at[i], rows_out.at[i], left_rows.at[i])

    def cols_leave(c):
        return pltpu.make_async_copy(cols_stage.at[c], cols_out.at[c], left_cols.at[c])

    def own(c):
        return [cols_in[c, a].astype(F32) for a in range(4)]

    def put(ref, c, first, values):
        for a, x in enumerate(values):
            ref[c, first + a] = x.astype(ref.dtype)

    def pair(buf, c):
        return (buf[c, 0].astype(F32), buf[c, 1].astype(F32))

    def body(c):
        @pl.when(c % QUARTERS == 0)
        def _():
            row_piece(rows_in, acc, rows_stage, c // QUARTERS, 1, tokens, depth)

        @pl.when(c % QUARTERS == 2)
        def _():
            row_piece(rows_in, acc, rows_stage, c // QUARTERS, 0, tokens, depth)
            rows_leave(c // QUARTERS).start()

        @pl.when(me == 0)
        def _():
            q, k, v, g = own(c)
            outs, grads = column_block([(q, g, 1)], [(k, v)], scaling)
            put(cols_stage, c, 0, outs[0])
            put(own_grads, c, 0, grads[0])

        @pl.when(me == 1)
        def _():
            kv_to(c, 1, in_a, got_a, 1).wait_recv()
            q, k, v, g = own(c)
            outs, grads = column_block([(q, g, 2)], [pair(in_a, c), (k, v)], scaling)
            put(in_a, c, 0, grads[0])
            ret_a_copy(c, in_a, 0, 0).start()
            put(cols_stage, c, 0, outs[0])
            put(own_grads, c, 0, grads[1])

        @pl.when(me == 2)
        def _():
            kv_to(c, 2, in_a, got_a, 0).wait_recv()
            kv_to(c, 2, in_b, got_b, 0).wait_recv()
            all_to(c).wait_recv()
            q, k, v, g = own(c)
            q3, k3, v3, g3 = [in_c[c, a].astype(F32) for a in range(4)]
            outs, grads = column_block(
                [(q, g, 3), (q3, g3, 4)],
                [pair(in_a, c), pair(in_b, c), (k, v), (k3, v3)],
                scaling,
            )
            put(in_a, c, 0, grads[0])
            put(in_b, c, 0, grads[1])
            put(in_c, c, 0, outs[1] + grads[3])
            ret_b_copy(c).start()
            ret_a_copy(c, in_b, 1, 1).start()
            ret_c_copy(c).start()
            put(cols_stage, c, 0, outs[0] + grads[2])
            cols_leave(c).start()

    each(chunks, body)

    @pl.when(me == 0)
    def _():
        def take(c):
            ret_a_copy(c, in_a, 0, 0).wait_recv()
            ret_b_copy(c).wait_recv()
            total = [
                own_grads[c, a] + ret_a[c, a].astype(F32) + ret_b[c, a].astype(F32)
                for a in range(2)
            ]
            put(cols_stage, c, 2, total)
            cols_leave(c).start()

        each(chunks, take)

    @pl.when(me == 1)
    def _():
        def take(c):
            ret_a_copy(c, in_b, 1, 1).wait_recv()
            put(cols_stage, c, 2, [own_grads[c, a] + ret_a[c, a].astype(F32) for a in range(2)])
            cols_leave(c).start()

        each(chunks, take)

    @pl.when(me == 3)
    def _():
        def take(c):
            ret_c_copy(c).wait_recv()
            cols_stage[c] = ret_c[c]
            cols_leave(c).start()

        each(chunks, take)

    each(heads, lambda i: rows_leave(i).wait())
    each(chunks, lambda c: cols_leave(c).wait())

    @pl.when(me == 0)
    def _():
        def done(c):
            kv_to(c, 2, in_a, got_a, 0).wait_send()
            kv_to(c, 1, in_a, got_a, 1).wait_send()

        each(chunks, done)

    @pl.when(me == 1)
    def _():
        def done(c):
            kv_to(c, 2, in_b, got_b, 0).wait_send()
            ret_a_copy(c, in_a, 0, 0).wait_send()

        each(chunks, done)

    @pl.when(me == 2)
    def _():
        def done(c):
            ret_b_copy(c).wait_send()
            ret_a_copy(c, in_b, 1, 1).wait_send()
            ret_c_copy(c).wait_send()

        each(chunks, done)

    @pl.when(me == 3)
    def _():
        each(chunks, lambda c: all_to(c).wait_send())


def join_kernel(
    rows_ref, cols_ref, o_out, dq_out, dk_out, dv_out, rows, cols, wide, joined, arrive, leave
):
    tokens, local_heads, depth = o_out.shape
    heads = local_heads // 2
    columns = tokens // QUARTERS
    outs = (o_out, dq_out, dk_out, dv_out)

    def rows_in(quarter):
        part = pl.ds(quarter * columns, columns)
        return pltpu.make_async_copy(
            rows_ref.at[:, :, part], rows.at[:, :, part], arrive.at[0, quarter]
        )

    def cols_in(quarter):
        part = pl.ds(quarter * heads, heads)
        return pltpu.make_async_copy(cols_ref.at[part], cols.at[part], arrive.at[1, quarter])

    def out(a, quarter):
        part = pl.ds(quarter * columns, columns)
        return pltpu.make_async_copy(joined.at[a, part], outs[a].at[part], leave.at[a, quarter])

    for quarter in range(QUARTERS):
        rows_in(quarter).start()
        cols_in(quarter).start()
    for quarter in range(QUARTERS):
        rows_in(quarter).wait()
        cols_in(quarter).wait()
        part = pl.ds(quarter * columns, columns)
        for a in range(4):
            for h in range(local_heads):
                x = rows[h // 2, a, part] if h % 2 == 0 else cols[quarter * heads + h // 2, a]
                wide[a, pl.ds(h, columns, stride=local_heads)] = x.astype(F32)
            joined[a, part] = wide[a].reshape(columns, local_heads, depth).astype(BF16)
            out(a, quarter).start()
    for quarter in range(QUARTERS):
        for a in range(4):
            out(a, quarter).wait()


def fused(queries, key_vecs, value_vecs, grad_out):
    shape = queries.shape
    tokens, local_heads, depth = shape[2:]
    heads = local_heads // 2
    columns = tokens // QUARTERS
    chunks = heads * QUARTERS
    flat = [x.reshape(tokens, local_heads, depth) for x in (queries, key_vecs, value_vecs, grad_out)]
    anywhere = pl.BlockSpec(memory_space=pl.ANY)
    two = pltpu.VMEM((chunks, 2, columns, depth), BF16)
    four = pltpu.VMEM((chunks, 4, columns, depth), BF16)
    row_buf = pltpu.VMEM((heads, 4, tokens, depth), BF16)
    dma = pltpu.SemaphoreType.DMA
    rows, cols = pl.pallas_call(
        kernel,
        out_shape=[
            jax.ShapeDtypeStruct((heads, 4, tokens, depth), BF16),
            jax.ShapeDtypeStruct((chunks, 4, columns, depth), BF16),
        ],
        in_specs=[anywhere] * 4,
        out_specs=[anywhere] * 2,
        scratch_shapes=[
            pltpu.VMEM((4, tokens, local_heads, depth), BF16),
            pltpu.VMEM((4, columns * local_heads, depth), F32),
            row_buf, four, row_buf, four,
            pltpu.VMEM((2, tokens // 2, depth), F32),
            pltpu.VMEM((chunks, 2, columns, depth), F32),
            two, two, four, two, two, four,
            dma((4, QUARTERS)),
            dma((2, chunks)), dma((chunks,)), dma((chunks,)), dma((chunks,)),
            dma((3, chunks)), dma((chunks,)), dma((chunks,)), dma((chunks,)),
            dma((heads,)), dma((chunks,)),
        ],
        compiler_params=pltpu.CompilerParams(
            collective_id=0, has_side_effects=True, vmem_limit_bytes=56 * 1024 * 1024
        ),
    )(*flat)
    results = pl.pallas_call(
        join_kernel,
        out_shape=[jax.ShapeDtypeStruct((tokens, local_heads, depth), BF16)] * 4,
        in_specs=[anywhere] * 2,
        out_specs=[anywhere] * 4,
        scratch_shapes=[
            row_buf, four,
            pltpu.VMEM((4, columns * local_heads, depth), F32),
            pltpu.VMEM((4, tokens, local_heads, depth), BF16),
            dma((2, QUARTERS)), dma((4, QUARTERS)),
        ],
        compiler_params=pltpu.CompilerParams(vmem_limit_bytes=60 * 1024 * 1024),
    )(rows, cols)
    return tuple(x.reshape(shape) for x in results)


def causal(length):
    positions = jnp.arange(length)
    return positions[None, :] <= positions[:, None]


def attend(query_in, key_in, value_in, grad_in, layout, allowed):
    scaling = 1.0 / math.sqrt(query_in.shape[-1])
    key_form = layout.replace("q", "k")
    scores = (
        jnp.einsum(
            layout + "," + key_form + "->bxhqk",
            query_in,
            key_in,
            preferred_element_type=jnp.float32,
        )
        * scaling
    )
    scores = jnp.where(allowed, scores, -1e30)
    highest = jnp.max(scores, axis=-1, keepdims=True)
    weight_sum = jnp.sum(jnp.exp(scores - highest), axis=-1, keepdims=True)
    log_total = highest + jnp.log(weight_sum)
    weights = jnp.where(allowed, jnp.exp(scores - log_total), 0.0)
    rounded = weights.astype(jnp.bfloat16)
    output = jnp.einsum(
        "bxhqk," + key_form + "->" + layout, rounded, value_in, preferred_element_type=jnp.float32
    ).astype(jnp.bfloat16)
    row_dots = jnp.einsum(
        layout + "," + layout + "->bxhq", grad_in, output, preferred_element_type=jnp.float32
    )
    dprobs = jnp.einsum(
        layout + "," + key_form + "->bxhqk", grad_in, value_in, preferred_element_type=jnp.float32
    )
    dscores = (weights * (dprobs - row_dots[..., None]) * scaling).astype(jnp.bfloat16)
    grad_query = jnp.einsum(
        "bxhqk," + key_form + "->" + layout, dscores, key_in, preferred_element_type=jnp.float32
    ).astype(jnp.bfloat16)
    grad_key = jnp.einsum(
        "bxhqk," + layout + "->" + key_form, dscores, query_in, preferred_element_type=jnp.float32
    )
    grad_value = jnp.einsum(
        "bxhqk," + layout + "->" + key_form, rounded, grad_in, preferred_element_type=jnp.float32
    )
    return (output, grad_query, grad_key, grad_value)


def merge_heads(first_part, second_part):
    stacked = jnp.stack((first_part, second_part), axis=4)
    shape = first_part.shape
    return stacked.reshape(shape[:3] + (2 * shape[3], shape[4]))


def per_device(queries, key_vecs, value_vecs, grad_out):
    arrays = (queries, key_vecs, value_vecs, grad_out)
    row_parts = tuple((array[:, :, :, 0::2] for array in arrays))
    col_parts = tuple((array[:, :, :, 1::2] for array in arrays))
    row_local = attend(
        row_parts[0], row_parts[1], row_parts[2], row_parts[3], "bxqhd", causal(queries.shape[2])
    )
    row_results = (
        row_local[0],
        row_local[1],
        row_local[2].astype(jnp.bfloat16),
        row_local[3].astype(jnp.bfloat16),
    )
    local_rows = col_parts[0].shape[1]
    gathered = (
        lax.all_gather(col_parts[1], "ctx", axis=1, tiled=True),
        lax.all_gather(col_parts[2], "ctx", axis=1, tiled=True),
    )
    query_rows = lax.axis_index("ctx") * local_rows + jnp.arange(local_rows)
    key_rows = jnp.arange(gathered[0].shape[1])
    allowed = key_rows[None, :] <= query_rows[:, None]
    col_local = attend(col_parts[0], gathered[0], gathered[1], col_parts[3], "bqxhd", allowed)
    summed = (
        lax.psum_scatter(col_local[2], "ctx", scatter_dimension=1, tiled=True),
        lax.psum_scatter(col_local[3], "ctx", scatter_dimension=1, tiled=True),
    )
    col_results = (
        col_local[0],
        col_local[1],
        summed[0].astype(jnp.bfloat16),
        summed[1].astype(jnp.bfloat16),
    )
    return (
        merge_heads(row_results[0], col_results[0]),
        merge_heads(row_results[1], col_results[1]),
        merge_heads(row_results[2], col_results[2]),
        merge_heads(row_results[3], col_results[3]),
    )


def solution(mesh):
    body = fused if mesh.shape["ctx"] == 4 else per_device
    placed = (
        P(("groups", "dp"), "ctx", None, "head", None),
        P(("groups", "dp"), "ctx", None, "head", None),
        P(("groups", "dp"), "ctx", None, "head", None),
        P(("groups", "dp"), "ctx", None, "head", None),
    )
    return jax.shard_map(
        body,
        mesh=mesh,
        in_specs=placed,
        out_specs=(
            P(("groups", "dp"), "ctx", None, "head", None),
            P(("groups", "dp"), "ctx", None, "head", None),
            P(("groups", "dp"), "ctx", None, "head", None),
            P(("groups", "dp"), "ctx", None, "head", None),
        ),
        check_vma=False,
    )
```
